256 devices in a mesh: rep: 4 (over y), dev: 64 (over z, x, core).
Axes of the slice: x: 4, y: 4, z: 8, core: 2. Of those that a mesh axis runs over, the one named last changes fastest.
Arguments:
- theta: bfloat16 [24, 2816, 1024], P(None, 'dev'), may hold values from -6 to 6
- deltas: bfloat16 [4, 24, 2816, 1024], P('rep', None, 'dev'), may hold values from -6 to 6
- momentum: float32 [128, 64, 4, 11, 1024], P('dev', None, 'rep'), may hold values from -2 to 2
- basis: bfloat16 [1024, 64], replicated, may hold values from -0.1875 to 0.1875
- slot_matrix: int32 [128], replicated, may hold values from -1 to 23, as said below
Outputs:
- new_theta: bfloat16 [24, 2816, 1024], P(None, 'dev')
The draws below stay inside these ranges and needn't reach their ends.
Inputs may be any that keep to these rules, and one draw needn't show every extreme that they name: `slot_matrix`: every matrix 0 to 23 stands in exactly one slot; -1 marks an empty slot; some device fills all 2 of its slots.
All inputs are finite; a program needn't handle non-finite values.
Results may differ from the reference program's by a relative error of at most 0.007.
Values may be sent and summed in bfloat16 or wider, within the bound.
A program may use at most 128 MiB of HBM per device.

```python
import jax
import jax.numpy as jnp
from jax import lax

MODEL_WIDTH = 1024
FF = 2816
RANK = 64
M = 24
OWNER_SLOTS = 2
TOTAL_SLOTS = 128
PIECE_ROWS = 11
N_REP = 4
N_DEV = 64


def draw_slot_matrix(key, part):
    key_full, slot_key, key_mat = jax.random.split(jax.random.fold_in(key, 7), 3)
    device_total = TOTAL_SLOTS // OWNER_SLOTS
    complete_device = jax.random.randint(key_full, (), 0, device_total).astype(jnp.int32)
    score_values = jax.random.permutation(slot_key, TOTAL_SLOTS).astype(jnp.int32)
    holder_owner = jnp.arange(TOTAL_SLOTS, dtype=jnp.int32) // OWNER_SLOTS
    score_values = score_values + TOTAL_SLOTS * (holder_owner == complete_device).astype(jnp.int32)
    order = jnp.argsort(-score_values).astype(jnp.int32)
    mat_order = jax.random.permutation(key_mat, M).astype(jnp.int32)
    lookup_table = jnp.full((TOTAL_SLOTS,), -1, jnp.int32)
    return lookup_table.at[order[:M]].set(mat_order)


def block_scale(rng, dims, cuts, smallest, top_value):
    loudness, own = 1.0, jax.random.fold_in(rng, 6)
    for axis_at, shards_of in cuts:
        draws = jnp.exp(jax.random.uniform(jax.random.fold_in(own, axis_at), (shards_of,), jnp.float32, smallest / len(cuts), top_value / len(cuts)))
        loudness = loudness * jnp.repeat(draws, dims[axis_at] // shards_of).reshape([-1 if axis == axis_at else 1 for axis in range(len(dims))])
    return loudness


def noise(key, extent, spread, reach, cuts=(), kind=jnp.bfloat16):
    values = jax.random.normal(key, extent, jnp.float32) * spread
    if len(cuts) > 0:
        values = block_scale(key, extent, cuts, -0.22, 0.18) * values
    return jnp.clip(values, min=-reach, max=reach).astype(kind)


def setup_inputs(seed: int = 0) -> dict:
    splits = jax.random.split(jax.random.key(seed), 6)
    theta = noise(splits[0], (M, FF, MODEL_WIDTH), 1.0, 6.0, ((1, 64),))
    deltas = noise(splits[1], (N_REP, M, FF, MODEL_WIDTH), 1.0, 6.0, ((0, 4), (2, 64)))
    momentum = noise(splits[2], (TOTAL_SLOTS, N_DEV, N_REP, PIECE_ROWS, MODEL_WIDTH), 0.3, 2.0, ((0, 64), (2, 4)), jnp.float32)
    basis = noise(splits[3], (MODEL_WIDTH, RANK), MODEL_WIDTH ** -0.5, 0.1875)
    slot_matrix = draw_slot_matrix(jax.random.fold_in(splits[5], 71), 0)
    return dict(theta=theta, deltas=deltas, momentum=momentum, basis=basis, slot_matrix=slot_matrix)


momentum_rate = 0.9
outer_rate = 0.7


def reference(theta, deltas, momentum, basis, slot_matrix):
    basis_wide = basis.astype(jnp.float32)
    paired_match = slot_matrix[None, :] == jnp.arange(M, dtype=jnp.int32)[:, None]
    slot_position = jnp.sum(jnp.where(paired_match, jnp.arange(TOTAL_SLOTS, dtype=jnp.int32)[None, :], 0), axis=1).astype(jnp.int32)

    def update_matrix(index):
        layer_deltas = lax.dynamic_index_in_dim(deltas, index, 1, keepdims=False)
        compressed = jnp.einsum("rfd,dk->rfk", layer_deltas.astype(jnp.float32), basis_wide,
                                precision=lax.Precision.HIGHEST).astype(jnp.bfloat16)
        averaged = jnp.sum(compressed.astype(jnp.float32), axis=0) / N_REP
        outer = jnp.dot(averaged, basis_wide.T, precision=lax.Precision.HIGHEST)
        moment = lax.dynamic_index_in_dim(momentum, slot_position[index], 0, keepdims=False).reshape(FF, MODEL_WIDTH)
        renewed = momentum_rate * moment + outer
        update = (outer_rate * (outer + momentum_rate * renewed)).astype(jnp.bfloat16)
        current = lax.dynamic_index_in_dim(theta, index, 0, keepdims=False)
        return (current.astype(jnp.float32) - update.astype(jnp.float32)).astype(jnp.bfloat16)

    return lax.map(update_matrix, jnp.arange(M, dtype=jnp.int32))
```

```python
import jax
import jax.numpy as jnp
from jax import lax
from jax.sharding import PartitionSpec as P

momentum_rate = 0.9
outer_rate = 0.7


def per_device(theta, deltas, momentum, basis, slot_matrix):
    matrices, rows, width = theta.shape
    slots, dev_count = momentum.shape[0], momentum.shape[1]
    piece = momentum.shape[3]
    rank = basis.shape[1]
    rep_count = lax.axis_size("rep")

    moment = momentum.reshape(slots, dev_count, piece * width).astype(jnp.bfloat16)
    landed = lax.all_to_all(moment, "dev", split_axis=1, concat_axis=1, tiled=True)

    compressed = jnp.dot(
        deltas[0].reshape(matrices * rows, width), basis, preferred_element_type=jnp.float32
    ).astype(jnp.bfloat16)
    every = lax.all_gather(compressed, "rep", axis=0, tiled=False)
    averaged = jnp.sum(every.astype(jnp.float32), axis=0) / rep_count
    high = averaged.astype(jnp.bfloat16)
    low = (averaged - high.astype(jnp.float32)).astype(jnp.bfloat16)
    outer = jnp.dot(
        jnp.concatenate([high, low], axis=1),
        jnp.concatenate([basis, basis], axis=1).T,
        preferred_element_type=jnp.float32,
    ).reshape(matrices, rows, width)

    paired_match = slot_matrix[None, :] == jnp.arange(matrices, dtype=jnp.int32)[:, None]
    slot_position = jnp.sum(
        jnp.where(paired_match, jnp.arange(slots * dev_count, dtype=jnp.int32)[None, :], 0), axis=1
    )
    ordering = slot_position % slots * dev_count + slot_position // slots
    chosen = jnp.take(landed.reshape(slots * dev_count, piece * width), ordering, axis=0)
    spread = lax.all_gather(chosen.reshape(matrices, 1, piece * width), "rep", axis=1, tiled=True)
    moments = spread.reshape(matrices, rows, width).astype(jnp.float32)
    renewed = momentum_rate * moments + outer
    update = (outer_rate * (outer + momentum_rate * renewed)).astype(jnp.bfloat16)
    return (theta.astype(jnp.float32) - update.astype(jnp.float32)).astype(jnp.bfloat16)


def solution(mesh):
    placed = (
        P(None, "dev", None),
        P("rep", None, "dev", None),
        P("dev", None, "rep", None, None),
        P(),
        P(),
    )
    return jax.shard_map(
        per_device, mesh=mesh, in_specs=placed, out_specs=P(None, "dev", None), check_vma=False
    )
```

```python
import functools

import jax
import jax.numpy as jnp
from jax import lax
from jax.experimental import pallas as pl
from jax.experimental.pallas import tpu as pltpu
from jax.sharding import PartitionSpec as P

momentum_rate = 0.9
outer_rate = 0.7
MESH = pl.DeviceIdType.MESH
ROW = 8
DEPTH = 8
REPS = 4
CHUNKS = ((0, 3), (3, 3), (6, 3), (9, 2))


def route(
    cap, row_ref, pick_ref, mom_ref, deltas_ref, basis_ref, moments_ref, comp_ref,
    row_in, z_out, z_in, copy_sems, x_send, x_recv, z_send, z_recv, y_send, y_recv, c_send, c_recv,
):
    rep = lax.axis_index("rep")
    dev = lax.axis_index("dev")
    z, place = dev // ROW, lax.rem(dev, ROW)
    slots = mom_ref.shape[0]
    right, left = lax.rem(rep + 1, REPS), lax.rem(rep + 3, REPS)
    across = lax.rem(rep + 2, REPS)

    def row_peer(step):
        return lax.rem(place + step, ROW)

    def z_peer(step):
        return lax.rem(z + step, DEPTH)

    barrier = pltpu.get_barrier_semaphore()
    for step in range(1, ROW):
        pl.semaphore_signal(barrier, inc=1, device_id=(rep, z * ROW + row_peer(step)), device_id_type=MESH)
    for step in range(1, DEPTH):
        pl.semaphore_signal(barrier, inc=1, device_id=(rep, z_peer(step) * ROW + place), device_id_type=MESH)
    for peer in (right, left, across):
        pl.semaphore_signal(barrier, inc=1, device_id=(peer, dev), device_id_type=MESH)
    pl.semaphore_wait(barrier, ROW + DEPTH + 1)

    def x_copy(chunk, step):
        start, count = CHUNKS[chunk]
        return pltpu.make_async_remote_copy(
            src_ref=mom_ref.at[:, :, row_peer(step), pl.ds(start, count)],
            dst_ref=row_in[chunk].at[pl.ds(place * slots, slots)],
            send_sem=x_send.at[chunk, step - 1],
            recv_sem=x_recv.at[chunk, step - 1],
            device_id=(rep, z * ROW + row_peer(step)),
            device_id_type=MESH,
        )

    def own_copy(chunk):
        start, count = CHUNKS[chunk]
        return pltpu.make_async_copy(
            mom_ref.at[:, :, place, pl.ds(start, count)],
            row_in[chunk].at[pl.ds(place * slots, slots)],
            copy_sems.at[chunk],
        )

    def z_copy(chunk, step):
        return pltpu.make_async_remote_copy(
            src_ref=z_out[chunk].at[z_peer(step)],
            dst_ref=z_in[chunk].at[pl.ds(z * cap, cap)],
            send_sem=z_send.at[chunk, step - 1],
            recv_sem=z_recv.at[chunk, step - 1],
            device_id=(rep, z_peer(step) * ROW + place),
            device_id_type=MESH,
        )

    def y_copy(chunk, way, block, target):
        start, count = CHUNKS[chunk]
        return pltpu.make_async_remote_copy(
            src_ref=moments_ref.at[block, pl.ds(start, count)],
            dst_ref=moments_ref.at[block, pl.ds(start, count)],
            send_sem=y_send.at[chunk, way],
            recv_sem=y_recv.at[chunk, way],
            device_id=(target, dev),
            device_id_type=MESH,
        )

    def to_right(chunk):
        return y_copy(chunk, 0, rep, right)

    def to_left(chunk):
        return y_copy(chunk, 1, rep, left)

    def onward(chunk):
        if chunk % 2 == 0:
            return y_copy(chunk, 2, left, right)
        return y_copy(chunk, 2, right, left)

    def c_copy(way, target):
        return pltpu.make_async_remote_copy(
            src_ref=comp_ref.at[rep],
            dst_ref=comp_ref.at[rep],
            send_sem=c_send.at[way],
            recv_sem=c_recv.at[way],
            device_id=(target, dev),
            device_id_type=MESH,
        )

    for chunk in range(len(CHUNKS)):
        for step in range(1, ROW):
            x_copy(chunk, step).start()
        own_copy(chunk).start()

    half = comp_ref.shape[1]
    basis = basis_ref[...]
    nothing = jnp.zeros_like(basis)
    dims = (((1,), (1,)), ((), ()))
    comp_ref[rep] = (
        lax.dot_general(deltas_ref[:half], jnp.concatenate([basis, nothing], axis=0), dims, preferred_element_type=jnp.float32)
        + lax.dot_general(deltas_ref[half:], jnp.concatenate([nothing, basis], axis=0), dims, preferred_element_type=jnp.float32)
    ).astype(jnp.bfloat16)
    for way, target in enumerate((right, left, across)):
        c_copy(way, target).start()

    def stage_z(chunk):
        for step in range(1, ROW):
            x_copy(chunk, step).wait_recv()
        own_copy(chunk).wait()
        for slot in range(cap):
            z_out[chunk][:, slot] = row_in[chunk][row_ref[slot]]
        for step in range(1, DEPTH):
            z_copy(chunk, step).start()
        z_in[chunk][pl.ds(z * cap, cap)] = z_out[chunk][z]

    def stage_y(chunk):
        start, count = CHUNKS[chunk]
        for step in range(1, DEPTH):
            z_copy(chunk, step).wait_recv()
        for group in range(moments_ref.shape[2]):
            for line in range(count):
                tile = jnp.stack(
                    [z_in[chunk][pick_ref[group * 8 + m], line].astype(jnp.float32) for m in range(8)], axis=0
                )
                moments_ref[rep, start + line, group] = jnp.swapaxes(tile, 0, 1).astype(jnp.bfloat16)
        to_right(chunk).start()
        to_left(chunk).start()

    def stage_relay(chunk):
        if chunk % 2 == 0:
            to_right(chunk).wait_recv()
        else:
            to_left(chunk).wait_recv()
        onward(chunk).start()

    def stage_end(chunk):
        if chunk % 2 == 0:
            to_left(chunk).wait_recv()
        else:
            to_right(chunk).wait_recv()
        onward(chunk).wait_recv()

    total = len(CHUNKS)
    for tick in range(total + 2):
        if tick < total:
            stage_z(tick)
        if 0 <= tick - 1 < total:
            stage_y(tick - 1)
        if 0 <= tick - 2 < total:
            stage_relay(tick - 2)
    for way, target in enumerate((right, left, across)):
        c_copy(way, target).wait()
    for chunk in range(total):
        stage_end(chunk)
    for chunk in range(total):
        for step in range(1, ROW):
            x_copy(chunk, step).wait_send()
        for step in range(1, DEPTH):
            z_copy(chunk, step).wait_send()
        to_right(chunk).wait_send()
        to_left(chunk).wait_send()
        onward(chunk).wait_send()


def routed(cap, row_slots, picks, moment, deltas, basis_t):
    slots, _, _, piece, tiles, lanes = moment.shape
    matrices = picks.shape[0]
    rank = basis_t.shape[0]
    half = deltas.shape[0] // 2
    chunks = len(CHUNKS)
    smem = pl.BlockSpec(memory_space=pltpu.SMEM)
    vmem = pl.BlockSpec(memory_space=pltpu.VMEM)
    return pl.pallas_call(
        functools.partial(route, cap),
        name="route_%d" % cap,
        out_shape=(
            jax.ShapeDtypeStruct((REPS, piece, matrices // 8, tiles, 8, lanes), jnp.bfloat16),
            jax.ShapeDtypeStruct((REPS, half, 2 * rank), jnp.bfloat16),
        ),
        in_specs=[smem, smem, pl.BlockSpec(memory_space=pl.ANY), vmem, vmem],
        out_specs=(vmem, vmem),
        scratch_shapes=[
            [pltpu.VMEM((ROW * slots, DEPTH, n, tiles, lanes), jnp.bfloat16) for _, n in CHUNKS],
            [pltpu.VMEM((DEPTH, cap, n, tiles, lanes), jnp.bfloat16) for _, n in CHUNKS],
            [pltpu.VMEM((DEPTH * cap, n, tiles, lanes), jnp.bfloat16) for _, n in CHUNKS],
            pltpu.SemaphoreType.DMA((chunks,)),
            pltpu.SemaphoreType.DMA((chunks, ROW - 1)),
            pltpu.SemaphoreType.DMA((chunks, ROW - 1)),
            pltpu.SemaphoreType.DMA((chunks, DEPTH - 1)),
            pltpu.SemaphoreType.DMA((chunks, DEPTH - 1)),
            pltpu.SemaphoreType.DMA((chunks, 3)),
            pltpu.SemaphoreType.DMA((chunks, 3)),
            pltpu.SemaphoreType.DMA((3,)),
            pltpu.SemaphoreType.DMA((3,)),
        ],
        compiler_params=pltpu.CompilerParams(
            collective_id=cap, has_side_effects=True, vmem_limit_bytes=40 << 20
        ),
    )(row_slots, picks, moment, deltas, basis_t)


def narrow(wide_ref, narrow_ref):
    narrow_ref[...] = wide_ref[...].astype(jnp.bfloat16)


def narrowed(wide):
    rows, lanes = wide.shape
    steps = 8
    spec = pl.BlockSpec((rows // steps, lanes), lambda i: (i, 0))
    return pl.pallas_call(
        narrow,
        name="narrow",
        grid=(steps,),
        out_shape=jax.ShapeDtypeStruct(wide.shape, jnp.bfloat16),
        in_specs=[spec],
        out_specs=spec,
    )(wide)


def finish(theta_ref, moments_ref, comp_ref, basis_ref, out_ref):
    block = pl.program_id(0)
    piece, matrices, width = theta_ref.shape
    lanes = moments_ref.shape[-1]
    rows = piece * matrices
    start = pl.multiple_of(lax.rem(block, 2) * rows, 8)
    total = comp_ref[0, pl.ds(start, rows)].astype(jnp.float32)
    for rep in range(1, REPS):
        total += comp_ref[rep, pl.ds(start, rows)].astype(jnp.float32)
    averaged = total / REPS
    high = averaged.astype(jnp.bfloat16)
    low = (averaged - high.astype(jnp.float32)).astype(jnp.bfloat16)
    basis = basis_ref[block // 2]
    for tile in range(width // lanes):
        cut = pl.ds(tile * lanes, lanes)
        outer = jnp.dot(high, basis[:, tile * lanes:(tile + 1) * lanes], preferred_element_type=jnp.float32)
        outer += jnp.dot(low, basis[:, tile * lanes:(tile + 1) * lanes], preferred_element_type=jnp.float32)
        outer = outer.reshape(piece, matrices, lanes)
        moment = moments_ref[0, :, :, tile].astype(jnp.float32).reshape(piece, matrices, lanes)
        renewed = momentum_rate * moment + outer
        update = (outer_rate * (outer + momentum_rate * renewed)).astype(jnp.bfloat16)
        out_ref[:, :, cut] = (
            theta_ref[:, :, cut].astype(jnp.float32) - update.astype(jnp.float32)
        ).astype(jnp.bfloat16)


def finished(theta, moments, compressed, basis_pair):
    rows, matrices, width = theta.shape
    piece = rows // REPS
    return pl.pallas_call(
        finish,
        name="finish",
        grid=(REPS,),
        out_shape=jax.ShapeDtypeStruct(theta.shape, jnp.bfloat16),
        in_specs=[
            pl.BlockSpec((piece, matrices, width), lambda r: (r, 0, 0)),
            pl.BlockSpec((1,) + moments.shape[1:], lambda r: (r, 0, 0, 0, 0, 0)),
            pl.BlockSpec(compressed.shape, lambda r: (0, 0, 0)),
            pl.BlockSpec(basis_pair.shape, lambda r: (0, 0, 0)),
        ],
        out_specs=pl.BlockSpec((piece, matrices, width), lambda r: (r, 0, 0)),
    )(theta, moments, compressed, basis_pair)


def per_device(caps, theta, deltas, momentum, basis, slot_matrix):
    matrices, rows, width = theta.shape
    slots, dev_count = momentum.shape[0], momentum.shape[1]
    piece = momentum.shape[3]
    entries = slots * dev_count
    per_row = slots * ROW

    moment = narrowed(momentum.reshape(-1, 128)).reshape(slots, DEPTH, ROW, piece, width // 128, 128)
    by_row = deltas[0].transpose(1, 0, 2).reshape(rows * matrices, width)
    basis_t = basis.T
    nothing = jnp.zeros_like(basis_t)
    basis_pair = jnp.stack(
        [jnp.concatenate([basis_t, nothing], axis=0), jnp.concatenate([nothing, basis_t], axis=0)]
    )

    place = jnp.arange(entries, dtype=jnp.int32)
    filled = slot_matrix >= 0
    ahead = (place[None, :] // per_row == place[:, None] // per_row) & (place[None, :] < place[:, None])
    order = jnp.sum((ahead & filled[None, :]).astype(jnp.int32), axis=1)
    mine = filled & (place // per_row == lax.axis_index("dev") // ROW)
    row_slots = jnp.sum(
        jnp.where(mine[None, :] & (order[None, :] == jnp.arange(per_row, dtype=jnp.int32)[:, None]), place % per_row, 0), axis=1
    )
    match = slot_matrix[None, :] == jnp.arange(matrices, dtype=jnp.int32)[:, None]
    owner_row = jnp.sum(jnp.where(match, place // per_row, 0), axis=1)
    owner_order = jnp.sum(jnp.where(match, order, 0), axis=1)
    largest = jnp.max(jnp.where(filled, order, 0)) + 1

    def branch(cap):
        return lambda: routed(cap, row_slots[:cap], owner_row * cap + owner_order, moment, by_row, basis_t)

    if len(caps) == 1:
        moments, compressed = branch(caps[0])()
    else:
        which = sum((largest > cap).astype(jnp.int32) for cap in caps[:-1])
        moments, compressed = lax.switch(which, [branch(cap) for cap in caps])
    return finished(theta.transpose(1, 0, 2), moments, compressed, basis_pair).transpose(1, 0, 2)


def solution(mesh):
    placed = (
        P(None, "dev", None),
        P("rep", None, "dev", None),
        P("dev", None, "rep", None, None),
        P(),
        P(),
    )
    return jax.shard_map(
        functools.partial(per_device, (6, 16)),
        mesh=mesh, in_specs=placed, out_specs=P(None, "dev", None), check_vma=False,
    )
```

```python
import functools

import jax
import jax.numpy as jnp
from jax import lax
from jax.experimental import pallas as pl
from jax.experimental.pallas import tpu as pltpu
from jax.sharding import PartitionSpec as P

momentum_rate = 0.9
outer_rate = 0.7
MESH = pl.DeviceIdType.MESH
CORES = 2
WIDE = 4
DEPTH = 8
REPS = 4
CHUNKS = ((0, 3), (3, 3), (6, 3), (9, 2))
CAPS = ((3, 6), (4, 8), (4, 16))


def route(
    chip_cap, row_cap, table_ref, mom_ref, deltas_ref, basis_ref, theta_ref, out_ref,
    wide, core_out, chip_in, x_out, row_in, z_out, z_in, moments, comp, deltas, theta, outer,
    load_sem, core_send, core_recv, x_send, x_recv, z_send, z_recv, y_send, y_recv, c_send, c_recv,
):
    rep = lax.axis_index("rep")
    dev = lax.axis_index("dev")
    core, x, z = lax.rem(dev, CORES), lax.rem(dev // CORES, WIDE), dev // (CORES * WIDE)
    slots = mom_ref.shape[0]
    total = len(CHUNKS)
    right, left, across = (lax.rem(rep + step, REPS) for step in (1, 3, 2))
    partner = (rep, dev + 1 - 2 * core)

    def x_peer(step):
        return lax.rem(x + step, WIDE)

    def x_device(step):
        return (rep, (z * WIDE + x_peer(step)) * CORES + core)

    def z_peer(step):
        return lax.rem(z + step, DEPTH)

    def z_device(step):
        return (rep, (z_peer(step) * WIDE + x) * CORES + core)

    def wide_copy(chunk):
        start, count = CHUNKS[chunk]
        return pltpu.make_async_copy(
            mom_ref.at[:, :, :, :, pl.ds(start, count)], wide[chunk], load_sem.at[chunk]
        )

    deltas_copy = pltpu.make_async_copy(deltas_ref, deltas, load_sem.at[total])
    theta_copy = pltpu.make_async_copy(theta_ref, theta, load_sem.at[total + 1])
    for chunk in range(total):
        wide_copy(chunk).start()
    deltas_copy.start()
    theta_copy.start()

    barrier = pltpu.get_barrier_semaphore()
    peers = [partner]
    peers += [x_device(step) for step in range(1, WIDE)]
    peers += [z_device(step) for step in range(1, DEPTH)]
    peers += [(peer, dev) for peer in (right, left, across)]
    for peer in peers:
        pl.semaphore_signal(barrier, inc=1, device_id=peer, device_id_type=MESH)

    def remote(src, dst, send, recv, device):
        return pltpu.make_async_remote_copy(
            src_ref=src, dst_ref=dst, send_sem=send, recv_sem=recv, device_id=device, device_id_type=MESH
        )

    def core_copy(chunk):
        return remote(
            core_out[chunk], chip_in[chunk].at[pl.ds(core * slots, slots)],
            core_send.at[chunk], core_recv.at[chunk], partner,
        )

    def x_copy(chunk, step):
        return remote(
            x_out[chunk].at[x_peer(step)], row_in[chunk].at[pl.ds(x * chip_cap, chip_cap)],
            x_send.at[chunk, step - 1], x_recv.at[chunk, step - 1], x_device(step),
        )

    def z_copy(chunk, step):
        return remote(
            z_out[chunk].at[z_peer(step)], z_in[chunk].at[pl.ds(z * row_cap, row_cap)],
            z_send.at[chunk, step - 1], z_recv.at[chunk, step - 1], z_device(step),
        )

    def y_copy(chunk, way, block, target):
        start, count = CHUNKS[chunk]
        part = moments.at[block, pl.ds(start, count)]
        return remote(part, part, y_send.at[chunk, way], y_recv.at[chunk, way], (target, dev))

    def to_right(chunk):
        return y_copy(chunk, 0, rep, right)

    def to_left(chunk):
        return y_copy(chunk, 1, rep, left)

    def onward(chunk):
        if chunk % 2 == 0:
            return y_copy(chunk, 2, left, right)
        return y_copy(chunk, 2, right, left)

    def c_copy(way):
        target = (right, left, across)[way]
        return remote(comp.at[rep], comp.at[rep], c_send.at[way], c_recv.at[way], (target, dev))

    def stage_core(chunk):
        wide_copy(chunk).wait()
        for column in range(WIDE):
            core_out[chunk][:, column] = wide[chunk][:, :, column, 1 - core].astype(jnp.bfloat16)
        if chunk == 0:
            pl.semaphore_wait(barrier, len(peers))
        core_copy(chunk).start()
        for column in range(WIDE):
            chip_in[chunk][pl.ds(core * slots, slots), column] = wide[chunk][:, :, column, core].astype(jnp.bfloat16)

    def stage_x(chunk):
        core_copy(chunk).wait_recv()
        for slot in range(chip_cap):
            x_out[chunk][:, slot] = chip_in[chunk][table_ref[slot]]
        for step in range(1, WIDE):
            x_copy(chunk, step).start()
        row_in[chunk][pl.ds(x * chip_cap, chip_cap)] = x_out[chunk][x]

    def stage_z(chunk):
        for step in range(1, WIDE):
            x_copy(chunk, step).wait_recv()
        for slot in range(row_cap):
            code = table_ref[4 + slot]
            z_out[chunk][:, slot] = row_in[chunk][code // 4 * chip_cap + lax.rem(code, 4)]
        for step in range(1, DEPTH):
            z_copy(chunk, step).start()
        z_in[chunk][pl.ds(z * row_cap, row_cap)] = z_out[chunk][z]

    def stage_y(chunk):
        start, count = CHUNKS[chunk]
        for step in range(1, DEPTH):
            z_copy(chunk, step).wait_recv()
        for group in range(moments.shape[2]):
            codes = [table_ref[20 + group * 8 + m] for m in range(8)]
            picks = [code // 16 * row_cap + lax.rem(code, 16) for code in codes]
            for line in range(count):
                tile = jnp.stack([z_in[chunk][pick, line].astype(jnp.float32) for pick in picks], axis=0)
                moments[rep, start + line, group] = jnp.swapaxes(tile, 0, 1).astype(jnp.bfloat16)
        to_right(chunk).start()
        to_left(chunk).start()

    def stage_relay(chunk):
        if chunk % 2 == 0:
            to_right(chunk).wait_recv()
        else:
            to_left(chunk).wait_recv()
        onward(chunk).start()

    def stage_end(chunk):
        if chunk % 2 == 0:
            to_left(chunk).wait_recv()
        else:
            to_right(chunk).wait_recv()
        onward(chunk).wait_recv()
        start, count = CHUNKS[chunk]
        piece, matrices, lanes = moments.shape[1], theta.shape[1], moments.shape[-1]
        for block in range(REPS):
            lines = pl.ds(block * piece + start, count)
            for tile in range(moments.shape[3]):
                cut = pl.ds(tile * lanes, lanes)
                moment = moments[block, pl.ds(start, count), :, tile].astype(jnp.float32)
                moment = moment.reshape(count, matrices, lanes)
                grad = outer[lines, :, cut]
                renewed = momentum_rate * moment + grad
                update = (outer_rate * (grad + momentum_rate * renewed)).astype(jnp.bfloat16)
                out_ref[lines, :, cut] = (
                    theta[lines, :, cut].astype(jnp.float32) - update.astype(jnp.float32)
                ).astype(jnp.bfloat16)

    half = comp.shape[1]

    def project():
        deltas_copy.wait()
        basis = basis_ref[...]
        nothing = jnp.zeros_like(basis)
        dims = (((1,), (1,)), ((), ()))
        upper = jnp.concatenate([basis, nothing], axis=0)
        lower = jnp.concatenate([nothing, basis], axis=0)
        comp[rep] = (
            lax.dot_general(deltas[:half], upper, dims, preferred_element_type=jnp.float32)
            + lax.dot_general(deltas[half:], lower, dims, preferred_element_type=jnp.float32)
        ).astype(jnp.bfloat16)
        for way in range(3):
            c_copy(way).start()

    def expand():
        for way in range(3):
            c_copy(way).wait()
        theta_copy.wait()
        summed = comp[0].astype(jnp.float32)
        for block in range(1, REPS):
            summed += comp[block].astype(jnp.float32)
        averaged = summed / REPS
        high = averaged.astype(jnp.bfloat16)
        low = (averaged - high.astype(jnp.float32)).astype(jnp.bfloat16)
        both = jnp.concatenate([high, low], axis=1)
        basis = basis_ref[...]
        nothing = jnp.zeros_like(basis)
        rows, matrices, width = theta.shape
        for part in range(2):
            pair = [basis, nothing] if part == 0 else [nothing, basis]
            stacked = jnp.concatenate(pair + pair, axis=0)
            outer[pl.ds(part * rows // 2, rows // 2)] = jnp.dot(
                both, stacked, preferred_element_type=jnp.float32
            ).reshape(rows // 2, matrices, width)

    for chunk in range(total):
        stage_core(chunk)
        if chunk >= 1:
            stage_x(chunk - 1)
    stage_x(total - 1)
    project()
    for tick in range(total + 3):
        if tick < total:
            stage_z(tick)
        if tick == 1:
            expand()
        if 0 <= tick - 1 < total:
            stage_y(tick - 1)
        if 0 <= tick - 2 < total:
            stage_relay(tick - 2)
        if 0 <= tick - 3 < total:
            stage_end(tick - 3)
    for chunk in range(total):
        core_copy(chunk).wait_send()
        for step in range(1, WIDE):
            x_copy(chunk, step).wait_send()
        for step in range(1, DEPTH):
            z_copy(chunk, step).wait_send()
        to_right(chunk).wait_send()
        to_left(chunk).wait_send()
        onward(chunk).wait_send()


def routed(caps, number, table, moment, deltas, basis_t, theta):
    chip_cap, row_cap = caps
    slots, _, _, _, piece, tiles, lanes = moment.shape
    matrices = theta.shape[1]
    half = deltas.shape[0] // 2
    chunks = len(CHUNKS)
    anywhere = pl.BlockSpec(memory_space=pl.ANY)
    vmem = pl.BlockSpec(memory_space=pltpu.VMEM)

    def buffers(dtype, *lead):
        return [pltpu.VMEM(lead + (n, tiles, lanes), dtype) for _, n in CHUNKS]

    def pair(*shape):
        return [pltpu.SemaphoreType.DMA(shape), pltpu.SemaphoreType.DMA(shape)]

    return pl.pallas_call(
        functools.partial(route, chip_cap, row_cap),
        name="route_%d_%d" % caps,
        out_shape=jax.ShapeDtypeStruct(theta.shape, jnp.bfloat16),
        in_specs=[pl.BlockSpec(memory_space=pltpu.SMEM), anywhere, anywhere, vmem, anywhere],
        out_specs=vmem,
        scratch_shapes=[
            buffers(jnp.float32, slots, DEPTH, WIDE, CORES),
            buffers(jnp.bfloat16, slots, WIDE, DEPTH),
            buffers(jnp.bfloat16, CORES * slots, WIDE, DEPTH),
            buffers(jnp.bfloat16, WIDE, chip_cap, DEPTH),
            buffers(jnp.bfloat16, WIDE * chip_cap, DEPTH),
            buffers(jnp.bfloat16, DEPTH, row_cap),
            buffers(jnp.bfloat16, DEPTH * row_cap),
            pltpu.VMEM((REPS, piece, matrices // 8, tiles, 8, lanes), jnp.bfloat16),
            pltpu.VMEM((REPS, half, 2 * basis_t.shape[0]), jnp.bfloat16),
            pltpu.VMEM(deltas.shape, jnp.bfloat16),
            pltpu.VMEM(theta.shape, jnp.bfloat16),
            pltpu.VMEM(theta.shape, jnp.float32),
            pltpu.SemaphoreType.DMA((chunks + 2,)),
            *pair(chunks),
            *pair(chunks, WIDE - 1),
            *pair(chunks, DEPTH - 1),
            *pair(chunks, 3),
            *pair(3),
        ],
        compiler_params=pltpu.CompilerParams(
            collective_id=number, has_side_effects=True, vmem_limit_bytes=56 << 20
        ),
    )(table, moment, deltas, basis_t, theta)


def per_device(theta, deltas, momentum, basis, slot_matrix):
    matrices, rows, width = theta.shape
    slots, dev_count = momentum.shape[0], momentum.shape[1]
    piece = momentum.shape[3]
    entries = slots * dev_count
    per_chip = slots * CORES
    per_row = per_chip * WIDE

    moment = momentum.reshape(slots, DEPTH, WIDE, CORES, piece, width // 128, 128)
    by_row = deltas[0].transpose(1, 0, 2).reshape(rows * matrices, width)

    dev = lax.axis_index("dev")
    place = jnp.arange(entries, dtype=jnp.int32)
    chip, row = place // per_chip, place // per_row
    filled = slot_matrix >= 0
    before = filled[None, :] & (place[None, :] < place[:, None])
    in_chip = jnp.sum((before & (chip[None, :] == chip[:, None])).astype(jnp.int32), axis=1)
    in_row = jnp.sum((before & (row[None, :] == row[:, None])).astype(jnp.int32), axis=1)
    line = jnp.arange(per_chip + per_row + matrices, dtype=jnp.int32)[:, None]
    of_chip, of_row = line < per_chip, line < per_chip + per_row
    chosen = jnp.where(
        of_chip,
        filled & (chip == dev // CORES) & (in_chip == line),
        jnp.where(
            of_row,
            filled & (row == dev // (CORES * WIDE)) & (in_row == line - per_chip),
            slot_matrix == line - per_chip - per_row,
        ),
    )
    value = jnp.where(
        of_chip, place % per_chip, jnp.where(of_row, chip % WIDE * per_chip + in_chip, row * per_row + in_row)
    )
    table = jnp.sum(jnp.where(chosen, value, 0), axis=1)
    most_chip = jnp.max(jnp.where(filled, in_chip, 0)) + 1
    most_row = jnp.max(jnp.where(filled, in_row, 0)) + 1
    which = sum(((most_chip > a) | (most_row > b)).astype(jnp.int32) for a, b in CAPS[:-1])

    def branch(number):
        return lambda: routed(
            CAPS[number], number, table, moment, by_row, basis.T, theta.transpose(1, 0, 2)
        )

    return lax.switch(which, [branch(n) for n in range(len(CAPS))]).transpose(1, 0, 2)


def solution(mesh):
    placed = (
        P(None, "dev", None),
        P("rep", None, "dev", None),
        P("dev", None, "rep", None, None),
        P(),
        P(),
    )
    return jax.shard_map(
        per_device, mesh=mesh, in_specs=placed, out_specs=P(None, "dev", None), check_vma=False,
    )
```

```python
import functools

import jax
import jax.numpy as jnp
from jax import lax
from jax.experimental import pallas as pl
from jax.experimental.pallas import tpu as pltpu
from jax.sharding import PartitionSpec as P

momentum_rate = 0.9
outer_rate = 0.7
MESH = pl.DeviceIdType.MESH
CORES = 2
WIDE = 4
DEPTH = 8
REPS = 4
CHUNKS = ((0, 2), (2, 2), (4, 2), (6, 2), (8, 2), (10, 1))
CAPS = ((2, 5), (3, 6), (4, 8), (4, 16))
WINDOW = 2
X_STEPS = (2, 1, 3)
Z_STEPS = (4, 3, 5, 2, 6, 1, 7)


def route(
    chip_cap, row_cap, table_ref, mom_ref, deltas_ref, basis_ref, theta_ref, out_ref,
    wide, core_out, chip_in, x_out, row_in, z_out, z_in, moments, comp, deltas, theta, outer,
    load_sem, core_send, core_recv, x_send, x_recv, z_send, z_recv, y_send, y_recv, c_send, c_recv,
):
    rep = lax.axis_index("rep")
    dev = lax.axis_index("dev")
    core, x, z = lax.rem(dev, CORES), lax.rem(dev // CORES, WIDE), dev // (CORES * WIDE)
    slots = mom_ref.shape[0]
    total = len(CHUNKS)
    right, left, across = (lax.rem(rep + step, REPS) for step in (1, 3, 2))
    partner = (rep, dev + 1 - 2 * core)

    def x_peer(step):
        return lax.rem(x + step, WIDE)

    def x_device(step):
        return (rep, (z * WIDE + x_peer(step)) * CORES + core)

    def z_peer(step):
        return lax.rem(z + step, DEPTH)

    def z_device(step):
        return (rep, (z_peer(step) * WIDE + x) * CORES + core)

    def wide_copy(chunk):
        start, count = CHUNKS[chunk]
        return pltpu.make_async_copy(
            mom_ref.at[:, :, :, :, pl.ds(start, count)], wide[chunk], load_sem.at[chunk]
        )

    deltas_copy = pltpu.make_async_copy(deltas_ref, deltas, load_sem.at[total])
    theta_copy = pltpu.make_async_copy(theta_ref, theta, load_sem.at[total + 1])
    for chunk in range(total):
        wide_copy(chunk).start()
    deltas_copy.start()
    theta_copy.start()

    barrier = pltpu.get_barrier_semaphore()
    peers = [partner]
    peers += [x_device(step) for step in range(1, WIDE)]
    peers += [z_device(step) for step in range(1, DEPTH)]
    peers += [(peer, dev) for peer in (right, left, across)]
    for peer in peers:
        pl.semaphore_signal(barrier, inc=1, device_id=peer, device_id_type=MESH)

    def remote(src, dst, send, recv, device):
        return pltpu.make_async_remote_copy(
            src_ref=src, dst_ref=dst, send_sem=send, recv_sem=recv, device_id=device, device_id_type=MESH
        )

    def core_copy(chunk):
        return remote(
            core_out[chunk], chip_in[chunk].at[pl.ds(core * slots, slots)],
            core_send.at[chunk], core_recv.at[chunk], partner,
        )

    def x_copy(chunk, step):
        return remote(
            x_out[chunk].at[x_peer(step)], row_in[chunk].at[pl.ds(x * chip_cap, chip_cap)],
            x_send.at[chunk, step - 1], x_recv.at[chunk, step - 1], x_device(step),
        )

    def z_copy(chunk, step):
        return remote(
            z_out[chunk].at[z_peer(step)], z_in[chunk].at[pl.ds(z * row_cap, row_cap)],
            z_send.at[chunk, step - 1], z_recv.at[chunk, step - 1], z_device(step),
        )

    def y_copy(chunk, way, block, target):
        start, count = CHUNKS[chunk]
        part = moments.at[block, pl.ds(start, count)]
        return remote(part, part, y_send.at[chunk, way], y_recv.at[chunk, way], (target, dev))

    def to_right(chunk):
        return y_copy(chunk, 0, rep, right)

    def to_left(chunk):
        return y_copy(chunk, 1, rep, left)

    def onward(chunk):
        if chunk % 2 == 0:
            return y_copy(chunk, 2, left, right)
        return y_copy(chunk, 2, right, left)

    def c_copy(way):
        target = (right, left, across)[way]
        return remote(comp.at[rep], comp.at[rep], c_send.at[way], c_recv.at[way], (target, dev))

    def stage_core(chunk):
        wide_copy(chunk).wait()
        for column in range(WIDE):
            core_out[chunk][:, column] = wide[chunk][:, :, column, 1 - core].astype(jnp.bfloat16)
        if chunk == 0:
            pl.semaphore_wait(barrier, len(peers))
        core_copy(chunk).start()
        for column in range(WIDE):
            chip_in[chunk][pl.ds(core * slots, slots), column] = wide[chunk][:, :, column, core].astype(jnp.bfloat16)

    def stage_x(chunk):
        core_copy(chunk).wait_recv()
        for slot in range(chip_cap):
            x_out[chunk][:, slot] = chip_in[chunk][table_ref[slot]]
        for step in X_STEPS:
            x_copy(chunk, step).start()
        row_in[chunk][pl.ds(x * chip_cap, chip_cap)] = x_out[chunk][x]

    def stage_z(chunk):
        for step in range(1, WIDE):
            x_copy(chunk, step).wait_recv()
        for slot in range(row_cap):
            code = table_ref[4 + slot]
            z_out[chunk][:, slot] = row_in[chunk][code // 4 * chip_cap + lax.rem(code, 4)]
        for step in Z_STEPS:
            z_copy(chunk, step).start()
        z_in[chunk][pl.ds(z * row_cap, row_cap)] = z_out[chunk][z]

    def stage_y(chunk):
        start, count = CHUNKS[chunk]
        for step in range(1, DEPTH):
            z_copy(chunk, step).wait_recv()
        for group in range(moments.shape[2]):
            codes = [table_ref[20 + group * 8 + m] for m in range(8)]
            picks = [code // 16 * row_cap + lax.rem(code, 16) for code in codes]
            for line in range(count):
                tile = jnp.stack([z_in[chunk][pick, line].astype(jnp.float32) for pick in picks], axis=0)
                moments[rep, start + line, group] = jnp.swapaxes(tile, 0, 1).astype(jnp.bfloat16)
        to_right(chunk).start()
        to_left(chunk).start()

    def stage_relay(chunk):
        if chunk % 2 == 0:
            to_right(chunk).wait_recv()
        else:
            to_left(chunk).wait_recv()
        onward(chunk).start()

    def stage_end(chunk):
        if chunk % 2 == 0:
            to_left(chunk).wait_recv()
        else:
            to_right(chunk).wait_recv()
        onward(chunk).wait_recv()
        start, count = CHUNKS[chunk]
        piece, matrices, lanes = moments.shape[1], theta.shape[1], moments.shape[-1]
        for block in range(REPS):
            lines = pl.ds(block * piece + start, count)
            for tile in range(moments.shape[3]):
                cut = pl.ds(tile * lanes, lanes)
                moment = moments[block, pl.ds(start, count), :, tile].astype(jnp.float32)
                moment = moment.reshape(count, matrices, lanes)
                grad = outer[lines, :, cut]
                renewed = momentum_rate * moment + grad
                update = (outer_rate * (grad + momentum_rate * renewed)).astype(jnp.bfloat16)
                out_ref[lines, :, cut] = (
                    theta[lines, :, cut].astype(jnp.float32) - update.astype(jnp.float32)
                ).astype(jnp.bfloat16)

    half = comp.shape[1]

    def project():
        deltas_copy.wait()
        basis = basis_ref[...]
        nothing = jnp.zeros_like(basis)
        dims = (((1,), (1,)), ((), ()))
        upper = jnp.concatenate([basis, nothing], axis=0)
        lower = jnp.concatenate([nothing, basis], axis=0)
        comp[rep] = (
            lax.dot_general(deltas[:half], upper, dims, preferred_element_type=jnp.float32)
            + lax.dot_general(deltas[half:], lower, dims, preferred_element_type=jnp.float32)
        ).astype(jnp.bfloat16)
        for way in range(3):
            c_copy(way).start()

    def expand():
        for way in range(3):
            c_copy(way).wait()
        theta_copy.wait()
        summed = comp[0].astype(jnp.float32)
        for block in range(1, REPS):
            summed += comp[block].astype(jnp.float32)
        averaged = summed / REPS
        high = averaged.astype(jnp.bfloat16)
        low = (averaged - high.astype(jnp.float32)).astype(jnp.bfloat16)
        both = jnp.concatenate([high, low], axis=1)
        basis = basis_ref[...]
        nothing = jnp.zeros_like(basis)
        rows, matrices, width = theta.shape
        for part in range(2):
            pair = [basis, nothing] if part == 0 else [nothing, basis]
            stacked = jnp.concatenate(pair + pair, axis=0)
            outer[pl.ds(part * rows // 2, rows // 2)] = jnp.dot(
                both, stacked, preferred_element_type=jnp.float32
            ).reshape(rows // 2, matrices, width)

    for chunk in range(total):
        stage_core(chunk)
        if 1 <= chunk <= WINDOW:
            stage_x(chunk - 1)
    if WINDOW == total:
        stage_x(total - 1)
    project()
    for tick in range(total + 3):
        if tick < total:
            stage_z(tick)
            if tick + WINDOW < total:
                stage_x(tick + WINDOW)
        if tick == 1:
            expand()
        if 0 <= tick - 1 < total:
            stage_y(tick - 1)
        if 0 <= tick - 2 < total:
            stage_relay(tick - 2)
        if 0 <= tick - 3 < total:
            stage_end(tick - 3)
    for chunk in range(total):
        core_copy(chunk).wait_send()
        for step in range(1, WIDE):
            x_copy(chunk, step).wait_send()
        for step in range(1, DEPTH):
            z_copy(chunk, step).wait_send()
        to_right(chunk).wait_send()
        to_left(chunk).wait_send()
        onward(chunk).wait_send()


def routed(caps, number, table, moment, deltas, basis_t, theta):
    chip_cap, row_cap = caps
    slots, _, _, _, piece, tiles, lanes = moment.shape
    matrices = theta.shape[1]
    half = deltas.shape[0] // 2
    chunks = len(CHUNKS)
    anywhere = pl.BlockSpec(memory_space=pl.ANY)
    vmem = pl.BlockSpec(memory_space=pltpu.VMEM)

    def buffers(dtype, *lead):
        return [pltpu.VMEM(lead + (n, tiles, lanes), dtype) for _, n in CHUNKS]

    def pair(*shape):
        return [pltpu.SemaphoreType.DMA(shape), pltpu.SemaphoreType.DMA(shape)]

    return pl.pallas_call(
        functools.partial(route, chip_cap, row_cap),
        name="route_%d_%d" % caps,
        out_shape=jax.ShapeDtypeStruct(theta.shape, jnp.bfloat16),
        in_specs=[pl.BlockSpec(memory_space=pltpu.SMEM), anywhere, anywhere, vmem, anywhere],
        out_specs=vmem,
        scratch_shapes=[
            buffers(jnp.float32, slots, DEPTH, WIDE, CORES),
            buffers(jnp.bfloat16, slots, WIDE, DEPTH),
            buffers(jnp.bfloat16, CORES * slots, WIDE, DEPTH),
            buffers(jnp.bfloat16, WIDE, chip_cap, DEPTH),
            buffers(jnp.bfloat16, WIDE * chip_cap, DEPTH),
            buffers(jnp.bfloat16, DEPTH, row_cap),
            buffers(jnp.bfloat16, DEPTH * row_cap),
            pltpu.VMEM((REPS, piece, matrices // 8, tiles, 8, lanes), jnp.bfloat16),
            pltpu.VMEM((REPS, half, 2 * basis_t.shape[0]), jnp.bfloat16),
            pltpu.VMEM(deltas.shape, jnp.bfloat16),
            pltpu.VMEM(theta.shape, jnp.bfloat16),
            pltpu.VMEM(theta.shape, jnp.float32),
            pltpu.SemaphoreType.DMA((chunks + 2,)),
            *pair(chunks),
            *pair(chunks, WIDE - 1),
            *pair(chunks, DEPTH - 1),
            *pair(chunks, 3),
            *pair(3),
        ],
        compiler_params=pltpu.CompilerParams(
            collective_id=number, has_side_effects=True, vmem_limit_bytes=56 << 20
        ),
    )(table, moment, deltas, basis_t, theta)


def per_device(theta, deltas, momentum, basis, slot_matrix):
    matrices, rows, width = theta.shape
    slots, dev_count = momentum.shape[0], momentum.shape[1]
    piece = momentum.shape[3]
    entries = slots * dev_count
    per_chip = slots * CORES
    per_row = per_chip * WIDE

    moment = momentum.reshape(slots, DEPTH, WIDE, CORES, piece, width // 128, 128)
    by_row = deltas[0].transpose(1, 0, 2).reshape(rows * matrices, width)

    dev = lax.axis_index("dev")
    place = jnp.arange(entries, dtype=jnp.int32)
    chip, row = place // per_chip, place // per_row
    filled = slot_matrix >= 0
    before = filled[None, :] & (place[None, :] < place[:, None])
    in_chip = jnp.sum((before & (chip[None, :] == chip[:, None])).astype(jnp.int32), axis=1)
    in_row = jnp.sum((before & (row[None, :] == row[:, None])).astype(jnp.int32), axis=1)
    line = jnp.arange(per_chip + per_row + matrices, dtype=jnp.int32)[:, None]
    of_chip, of_row = line < per_chip, line < per_chip + per_row
    chosen = jnp.where(
        of_chip,
        filled & (chip == dev // CORES) & (in_chip == line),
        jnp.where(
            of_row,
            filled & (row == dev // (CORES * WIDE)) & (in_row == line - per_chip),
            slot_matrix == line - per_chip - per_row,
        ),
    )
    value = jnp.where(
        of_chip, place % per_chip, jnp.where(of_row, chip % WIDE * per_chip + in_chip, row * per_row + in_row)
    )
    table = jnp.sum(jnp.where(chosen, value, 0), axis=1)
    most_chip = jnp.max(jnp.where(filled, in_chip, 0)) + 1
    most_row = jnp.max(jnp.where(filled, in_row, 0)) + 1
    which = sum(((most_chip > a) | (most_row > b)).astype(jnp.int32) for a, b in CAPS[:-1])

    def branch(number):
        return lambda: routed(
            CAPS[number], number, table, moment, by_row, basis.T, theta.transpose(1, 0, 2)
        )

    return lax.switch(which, [branch(n) for n in range(len(CAPS))]).transpose(1, 0, 2)


def solution(mesh):
    placed = (
        P(None, "dev", None),
        P("rep", None, "dev", None),
        P("dev", None, "rep", None, None),
        P(),
        P(),
    )
    return jax.shard_map(
        per_device, mesh=mesh, in_specs=placed, out_specs=P(None, "dev", None), check_vma=False,
    )
```

```python
import functools

import jax
import jax.numpy as jnp
from jax import lax
from jax.experimental import pallas as pl
from jax.experimental.pallas import tpu as pltpu
from jax.sharding import PartitionSpec as P

momentum_rate = 0.9
outer_rate = 0.7
MESH = pl.DeviceIdType.MESH
CORES = 2
WIDE = 4
DEPTH = 8
REPS = 4
CHUNKS = ((0, 1), (1, 2), (3, 2), (5, 2), (7, 2), (9, 2))
CAPS = ((2, 5), (3, 6), (4, 8), (4, 16))
WINDOW = 2
X_STEPS = (2, 1, 3)
Z_STEPS = (4, 3, 5, 2, 6, 1, 7)


def route(
    chip_cap, row_cap, table_ref, mom_ref, deltas_ref, basis_ref, theta_ref, out_ref,
    wide, core_out, chip_in, x_out, row_in, z_out, z_in, moments, comp, deltas, theta, outer,
    load_sem, core_send, core_recv, x_send, x_recv, z_send, z_recv, y_send, y_recv, c_send, c_recv,
):
    rep = lax.axis_index("rep")
    dev = lax.axis_index("dev")
    core, x, z = lax.rem(dev, CORES), lax.rem(dev // CORES, WIDE), dev // (CORES * WIDE)
    slots = mom_ref.shape[0]
    total = len(CHUNKS)
    right, left, across = (lax.rem(rep + step, REPS) for step in (1, 3, 2))
    partner = (rep, dev + 1 - 2 * core)

    def x_peer(step):
        return lax.rem(x + step, WIDE)

    def x_device(step):
        return (rep, (z * WIDE + x_peer(step)) * CORES + core)

    def z_peer(step):
        return lax.rem(z + step, DEPTH)

    def z_device(step):
        return (rep, (z_peer(step) * WIDE + x) * CORES + core)

    def wide_copy(chunk):
        start, count = CHUNKS[chunk]
        return pltpu.make_async_copy(
            mom_ref.at[:, :, :, :, pl.ds(start, count)], wide[chunk], load_sem.at[chunk]
        )

    deltas_copy = pltpu.make_async_copy(deltas_ref, deltas, load_sem.at[total])
    theta_copy = pltpu.make_async_copy(theta_ref, theta, load_sem.at[total + 1])
    for chunk in range(total):
        wide_copy(chunk).start()
    deltas_copy.start()
    theta_copy.start()

    barrier = pltpu.get_barrier_semaphore()
    peers = [partner]
    peers += [x_device(step) for step in range(1, WIDE)]
    peers += [z_device(step) for step in range(1, DEPTH)]
    peers += [(peer, dev) for peer in (right, left, across)]
    for peer in peers:
        pl.semaphore_signal(barrier, inc=1, device_id=peer, device_id_type=MESH)

    def remote(src, dst, send, recv, device):
        return pltpu.make_async_remote_copy(
            src_ref=src, dst_ref=dst, send_sem=send, recv_sem=recv, device_id=device, device_id_type=MESH
        )

    def core_copy(chunk):
        return remote(
            core_out[chunk], chip_in[chunk].at[pl.ds(core * slots, slots)],
            core_send.at[chunk], core_recv.at[chunk], partner,
        )

    def x_copy(chunk, step):
        return remote(
            x_out[chunk].at[x_peer(step)], row_in[chunk].at[pl.ds(x * chip_cap, chip_cap)],
            x_send.at[chunk, step - 1], x_recv.at[chunk, step - 1], x_device(step),
        )

    def z_copy(chunk, step):
        return remote(
            z_out[chunk].at[z_peer(step)], z_in[chunk].at[pl.ds(z * row_cap, row_cap)],
            z_send.at[chunk, step - 1], z_recv.at[chunk, step - 1], z_device(step),
        )

    def y_copy(chunk, way, block, target):
        start, count = CHUNKS[chunk]
        part = moments.at[block, pl.ds(start, count)]
        return remote(part, part, y_send.at[chunk, way], y_recv.at[chunk, way], (target, dev))

    def to_right(chunk):
        return y_copy(chunk, 0, rep, right)

    def to_left(chunk):
        return y_copy(chunk, 1, rep, left)

    def onward(chunk):
        if chunk % 2 == 0:
            return y_copy(chunk, 2, left, right)
        return y_copy(chunk, 2, right, left)

    def c_copy(way):
        target = (right, left, across)[way]
        return remote(comp.at[rep], comp.at[rep], c_send.at[way], c_recv.at[way], (target, dev))

    def stage_core(chunk):
        wide_copy(chunk).wait()
        for column in range(WIDE):
            core_out[chunk][:, column] = wide[chunk][:, :, column, 1 - core].astype(jnp.bfloat16)
        if chunk == 0:
            pl.semaphore_wait(barrier, len(peers))
        core_copy(chunk).start()
        for column in range(WIDE):
            chip_in[chunk][pl.ds(core * slots, slots), column] = wide[chunk][:, :, column, core].astype(jnp.bfloat16)

    def stage_x(chunk):
        core_copy(chunk).wait_recv()
        for slot in range(chip_cap):
            x_out[chunk][:, slot] = chip_in[chunk][table_ref[0, slot]]
        for step in X_STEPS:
            x_copy(chunk, step).start()
        row_in[chunk][pl.ds(x * chip_cap, chip_cap)] = x_out[chunk][x]

    def stage_z(chunk):
        for step in range(1, WIDE):
            x_copy(chunk, step).wait_recv()
        for slot in range(row_cap):
            code = table_ref[0, 4 + slot]
            z_out[chunk][:, slot] = row_in[chunk][code // 4 * chip_cap + lax.rem(code, 4)]
        for step in Z_STEPS:
            z_copy(chunk, step).start()
        z_in[chunk][pl.ds(z * row_cap, row_cap)] = z_out[chunk][z]

    def stage_y(chunk):
        start, count = CHUNKS[chunk]
        for step in range(1, DEPTH):
            z_copy(chunk, step).wait_recv()
        for group in range(moments.shape[2]):
            codes = [table_ref[0, 20 + group * 8 + m] for m in range(8)]
            picks = [code // 16 * row_cap + lax.rem(code, 16) for code in codes]
            for line in range(count):
                tile = jnp.stack([z_in[chunk][pick, line].astype(jnp.float32) for pick in picks], axis=0)
                moments[rep, start + line, group] = jnp.swapaxes(tile, 0, 1).astype(jnp.bfloat16)
        to_right(chunk).start()
        to_left(chunk).start()

    def stage_relay(chunk):
        if chunk % 2 == 0:
            to_right(chunk).wait_recv()
        else:
            to_left(chunk).wait_recv()
        onward(chunk).start()

    def stage_end(chunk):
        if chunk % 2 == 0:
            to_left(chunk).wait_recv()
        else:
            to_right(chunk).wait_recv()
        onward(chunk).wait_recv()
        start, count = CHUNKS[chunk]
        piece, matrices, lanes = moments.shape[1], theta.shape[1], moments.shape[-1]
        for block in range(REPS):
            lines = pl.ds(block * piece + start, count)
            for tile in range(moments.shape[3]):
                cut = pl.ds(tile * lanes, lanes)
                moment = moments[block, pl.ds(start, count), :, tile].astype(jnp.float32)
                moment = moment.reshape(count, matrices, lanes)
                grad = outer[lines, :, cut]
                renewed = momentum_rate * moment + grad
                update = (outer_rate * (grad + momentum_rate * renewed)).astype(jnp.bfloat16)
                out_ref[lines, :, cut] = (
                    theta[lines, :, cut].astype(jnp.float32) - update.astype(jnp.float32)
                ).astype(jnp.bfloat16)

    half = comp.shape[1]

    def project():
        deltas_copy.wait()
        basis = basis_ref[...]
        nothing = jnp.zeros_like(basis)
        dims = (((1,), (1,)), ((), ()))
        upper = jnp.concatenate([basis, nothing], axis=0)
        lower = jnp.concatenate([nothing, basis], axis=0)
        comp[rep] = (
            lax.dot_general(deltas[:half], upper, dims, preferred_element_type=jnp.float32)
            + lax.dot_general(deltas[half:], lower, dims, preferred_element_type=jnp.float32)
        ).astype(jnp.bfloat16)
        for way in range(3):
            c_copy(way).start()

    def expand():
        for way in range(3):
            c_copy(way).wait()
        theta_copy.wait()
        summed = comp[0].astype(jnp.float32)
        for block in range(1, REPS):
            summed += comp[block].astype(jnp.float32)
        averaged = summed / REPS
        high = averaged.astype(jnp.bfloat16)
        low = (averaged - high.astype(jnp.float32)).astype(jnp.bfloat16)
        both = jnp.concatenate([high, low], axis=1)
        basis = basis_ref[...]
        nothing = jnp.zeros_like(basis)
        rows, matrices, width = theta.shape
        for part in range(2):
            pair = [basis, nothing] if part == 0 else [nothing, basis]
            stacked = jnp.concatenate(pair + pair, axis=0)
            outer[pl.ds(part * rows // 2, rows // 2)] = jnp.dot(
                both, stacked, preferred_element_type=jnp.float32
            ).reshape(rows // 2, matrices, width)

    for chunk in range(total):
        stage_core(chunk)
        if 1 <= chunk <= WINDOW:
            stage_x(chunk - 1)
    if WINDOW == total:
        stage_x(total - 1)
    project()
    for tick in range(total + 3):
        if tick < total:
            stage_z(tick)
            if tick + WINDOW < total:
                stage_x(tick + WINDOW)
        if tick == 1:
            expand()
        if 0 <= tick - 1 < total:
            stage_y(tick - 1)
        if 0 <= tick - 2 < total:
            stage_relay(tick - 2)
        if 0 <= tick - 3 < total:
            stage_end(tick - 3)
    for chunk in range(total):
        core_copy(chunk).wait_send()
        for step in range(1, WIDE):
            x_copy(chunk, step).wait_send()
        for step in range(1, DEPTH):
            z_copy(chunk, step).wait_send()
        to_right(chunk).wait_send()
        to_left(chunk).wait_send()
        onward(chunk).wait_send()


def routed(caps, number, table, moment, deltas, basis_t, theta):
    chip_cap, row_cap = caps
    slots, _, _, _, piece, tiles, lanes = moment.shape
    matrices = theta.shape[1]
    half = deltas.shape[0] // 2
    chunks = len(CHUNKS)
    anywhere = pl.BlockSpec(memory_space=pl.ANY)
    vmem = pl.BlockSpec(memory_space=pltpu.VMEM)

    def buffers(dtype, *lead):
        return [pltpu.VMEM(lead + (n, tiles, lanes), dtype) for _, n in CHUNKS]

    def pair(*shape):
        return [pltpu.SemaphoreType.DMA(shape), pltpu.SemaphoreType.DMA(shape)]

    return pl.pallas_call(
        functools.partial(route, chip_cap, row_cap),
        name="route_%d_%d" % caps,
        out_shape=jax.ShapeDtypeStruct(theta.shape, jnp.bfloat16),
        in_specs=[pl.BlockSpec(memory_space=pltpu.SMEM), anywhere, anywhere, vmem, anywhere],
        out_specs=vmem,
        scratch_shapes=[
            buffers(jnp.float32, slots, DEPTH, WIDE, CORES),
            buffers(jnp.bfloat16, slots, WIDE, DEPTH),
            buffers(jnp.bfloat16, CORES * slots, WIDE, DEPTH),
            buffers(jnp.bfloat16, WIDE, chip_cap, DEPTH),
            buffers(jnp.bfloat16, WIDE * chip_cap, DEPTH),
            buffers(jnp.bfloat16, DEPTH, row_cap),
            buffers(jnp.bfloat16, DEPTH * row_cap),
            pltpu.VMEM((REPS, piece, matrices // 8, tiles, 8, lanes), jnp.bfloat16),
            pltpu.VMEM((REPS, half, 2 * basis_t.shape[0]), jnp.bfloat16),
            pltpu.VMEM(deltas.shape, jnp.bfloat16),
            pltpu.VMEM(theta.shape, jnp.bfloat16),
            pltpu.VMEM(theta.shape, jnp.float32),
            pltpu.SemaphoreType.DMA((chunks + 2,)),
            *pair(chunks),
            *pair(chunks, WIDE - 1),
            *pair(chunks, DEPTH - 1),
            *pair(chunks, 3),
            *pair(3),
        ],
        compiler_params=pltpu.CompilerParams(
            collective_id=number, has_side_effects=True, vmem_limit_bytes=56 << 20
        ),
    )(table, moment, deltas, basis_t, theta)


def arrange(per_chip, per_row, matrices, slot_ref, table_ref, which_ref):
    dev = lax.axis_index("dev")
    entries = slot_ref.shape[1]
    square = (entries, entries)
    across = jnp.broadcast_to(slot_ref[...], square)
    down = across.T
    place = lax.broadcasted_iota(jnp.int32, square, 0)
    line = lax.broadcasted_iota(jnp.int32, square, 1)
    chip, row = place // per_chip, place // per_row
    before = (across >= 0) & (line < place)
    in_chip = jnp.sum(jnp.where(before & (line // per_chip == chip), 1, 0), axis=1, keepdims=True)
    in_row = jnp.sum(jnp.where(before & (line // per_row == row), 1, 0), axis=1, keepdims=True)
    filled = down >= 0
    of_chip, of_row = line < per_chip, line < per_chip + per_row
    in_mine = (chip == dev // CORES) & (in_chip == line)
    in_line = (row == dev // (CORES * WIDE)) & (in_row == line - per_chip)
    held = down == line - per_chip - per_row
    value = jnp.where(
        of_chip,
        jnp.where(filled & in_mine, place % per_chip, 0),
        jnp.where(
            of_row,
            jnp.where(filled & in_line, chip % WIDE * per_chip + in_chip, 0),
            jnp.where(filled & held, row * per_row + in_row, 0),
        ),
    )
    table_ref[...] = jnp.sum(value, axis=0, keepdims=True)
    needed = jnp.zeros(square, jnp.int32)
    for chip_cap, row_cap in CAPS[:-1]:
        needed += jnp.where((in_chip >= chip_cap) | (in_row >= row_cap), 1, 0)
    which_ref[0, 0] = jnp.max(jnp.where(filled, needed, 0))


def planned(slot_row, per_chip, per_row, matrices):
    return pl.pallas_call(
        functools.partial(arrange, per_chip, per_row, matrices),
        name="arrange",
        out_shape=(
            jax.ShapeDtypeStruct(slot_row.shape, jnp.int32),
            jax.ShapeDtypeStruct((1, 1), jnp.int32),
        ),
        in_specs=[pl.BlockSpec(memory_space=pltpu.VMEM)],
        out_specs=(pl.BlockSpec(memory_space=pltpu.VMEM), pl.BlockSpec(memory_space=pltpu.SMEM)),
    )(slot_row)


def per_device(theta, deltas, momentum, basis, slot_matrix):
    matrices, rows, width = theta.shape
    slots, dev_count = momentum.shape[0], momentum.shape[1]
    piece = momentum.shape[3]
    entries = slots * dev_count
    per_chip = slots * CORES
    per_row = per_chip * WIDE

    moment = momentum.reshape(slots, DEPTH, WIDE, CORES, piece, width // 128, 128)
    by_row = deltas[0].transpose(1, 0, 2).reshape(rows * matrices, width)

    table, which = planned(slot_matrix.reshape(1, entries), per_chip, per_row, matrices)

    def branch(number):
        return lambda: routed(
            CAPS[number], number, table, moment, by_row, basis.T, theta.transpose(1, 0, 2)
        )

    return lax.switch(which.reshape(()), [branch(n) for n in range(len(CAPS))]).transpose(1, 0, 2)


def solution(mesh):
    placed = (
        P(None, "dev", None),
        P("rep", None, "dev", None),
        P("dev", None, "rep", None, None),
        P(),
        P(),
    )
    return jax.shard_map(
        per_device, mesh=mesh, in_specs=placed, out_specs=P(None, "dev", None), check_vma=False,
    )
```

```python
import functools

import jax
import jax.numpy as jnp
from jax import lax
from jax.experimental import pallas as pl
from jax.experimental.pallas import tpu as pltpu
from jax.sharding import PartitionSpec as P

momentum_rate = 0.9
outer_rate = 0.7
MESH = pl.DeviceIdType.MESH
CORES = 2
WIDE = 4
DEPTH = 8
REPS = 4
CHUNKS = ((0, 1), (1, 2), (3, 2), (5, 2), (7, 2), (9, 2))
CAPS = ((2, 5), (3, 6), (4, 8), (4, 16))
WINDOW = 2
X_STEPS = (2, 1, 3)
Z_STEPS = (4, 3, 5, 2, 6, 1, 7)


def route(
    chip_cap, row_cap, table_ref, mom_ref, deltas_ref, basis_ref, theta_ref, out_ref,
    wide, core_out, chip_in, x_out, row_in, z_out, z_in, moments, comp, deltas, theta, outer,
    load_sem, core_send, core_recv, x_send, x_recv, z_send, z_recv, y_send, y_recv, c_send, c_recv,
):
    rep = lax.axis_index("rep")
    dev = lax.axis_index("dev")
    core, x, z = lax.rem(dev, CORES), lax.rem(dev // CORES, WIDE), dev // (CORES * WIDE)
    slots = mom_ref.shape[0]
    total = len(CHUNKS)
    right, left, across = (lax.rem(rep + step, REPS) for step in (1, 3, 2))
    partner = (rep, dev + 1 - 2 * core)

    def x_peer(step):
        return lax.rem(x + step, WIDE)

    def x_device(step):
        return (rep, (z * WIDE + x_peer(step)) * CORES + core)

    def z_peer(step):
        return lax.rem(z + step, DEPTH)

    def z_device(step):
        return (rep, (z_peer(step) * WIDE + x) * CORES + core)

    def wide_copy(chunk):
        start, count = CHUNKS[chunk]
        return pltpu.make_async_copy(
            mom_ref.at[:, :, :, :, pl.ds(start, count)], wide[chunk], load_sem.at[chunk]
        )

    deltas_copy = pltpu.make_async_copy(deltas_ref, deltas, load_sem.at[total])
    theta_copy = pltpu.make_async_copy(theta_ref, theta, load_sem.at[total + 1])
    for chunk in range(total):
        wide_copy(chunk).start()
    deltas_copy.start()
    theta_copy.start()

    barrier = pltpu.get_barrier_semaphore()
    peers = [partner]
    peers += [x_device(step) for step in range(1, WIDE)]
    peers += [z_device(step) for step in range(1, DEPTH)]
    peers += [(peer, dev) for peer in (right, left, across)]
    for peer in peers:
        pl.semaphore_signal(barrier, inc=1, device_id=peer, device_id_type=MESH)

    def remote(src, dst, send, recv, device):
        return pltpu.make_async_remote_copy(
            src_ref=src, dst_ref=dst, send_sem=send, recv_sem=recv, device_id=device, device_id_type=MESH
        )

    def core_copy(chunk):
        return remote(
            core_out[chunk], chip_in[chunk].at[pl.ds(core * slots, slots)],
            core_send.at[chunk], core_recv.at[chunk], partner,
        )

    def x_copy(chunk, step):
        return remote(
            x_out[chunk].at[x_peer(step)], row_in[chunk].at[pl.ds(x * chip_cap, chip_cap)],
            x_send.at[chunk, step - 1], x_recv.at[chunk, step - 1], x_device(step),
        )

    def z_copy(chunk, step):
        return remote(
            z_out[chunk].at[z_peer(step)], z_in[chunk].at[pl.ds(z * row_cap, row_cap)],
            z_send.at[chunk, step - 1], z_recv.at[chunk, step - 1], z_device(step),
        )

    def y_copy(chunk, way, block, target):
        start, count = CHUNKS[chunk]
        part = moments.at[block, pl.ds(start, count)]
        return remote(part, part, y_send.at[chunk, way], y_recv.at[chunk, way], (target, dev))

    def to_right(chunk):
        return y_copy(chunk, 0, rep, right)

    def to_left(chunk):
        return y_copy(chunk, 1, rep, left)

    def onward(chunk):
        if chunk % 2 == 0:
            return y_copy(chunk, 2, left, right)
        return y_copy(chunk, 2, right, left)

    def c_copy(way):
        target = (right, left, across)[way]
        return remote(comp.at[rep], comp.at[rep], c_send.at[way], c_recv.at[way], (target, dev))

    def stage_core(chunk):
        wide_copy(chunk).wait()
        for column in range(WIDE):
            core_out[chunk][:, column] = wide[chunk][:, :, column, 1 - core].astype(jnp.bfloat16)
        if chunk == 0:
            pl.semaphore_wait(barrier, len(peers))
        core_copy(chunk).start()
        for column in range(WIDE):
            chip_in[chunk][pl.ds(core * slots, slots), column] = wide[chunk][:, :, column, core].astype(jnp.bfloat16)

    def stage_x(chunk):
        core_copy(chunk).wait_recv()
        for slot in range(chip_cap):
            x_out[chunk][:, slot] = chip_in[chunk][table_ref[0, slot]]
        for step in X_STEPS:
            x_copy(chunk, step).start()
        row_in[chunk][pl.ds(x * chip_cap, chip_cap)] = x_out[chunk][x]

    def stage_z(chunk):
        for step in range(1, WIDE):
            x_copy(chunk, step).wait_recv()
        for slot in range(row_cap):
            code = table_ref[0, 4 + slot]
            z_out[chunk][:, slot] = row_in[chunk][code // 4 * chip_cap + lax.rem(code, 4)]
        for step in Z_STEPS:
            z_copy(chunk, step).start()
        z_in[chunk][pl.ds(z * row_cap, row_cap)] = z_out[chunk][z]

    def stage_y(chunk):
        start, count = CHUNKS[chunk]
        for step in range(1, DEPTH):
            z_copy(chunk, step).wait_recv()
        for group in range(moments.shape[2]):
            codes = [table_ref[0, 20 + group * 8 + m] for m in range(8)]
            picks = [code // 16 * row_cap + lax.rem(code, 16) for code in codes]
            for line in range(count):
                tile = jnp.stack([z_in[chunk][pick, line].astype(jnp.float32) for pick in picks], axis=0)
                moments[rep, start + line, group] = jnp.swapaxes(tile, 0, 1).astype(jnp.bfloat16)
        first, second = (to_right, to_left) if chunk % 2 == 0 else (to_left, to_right)
        first(chunk).start()
        second(chunk).start()

    def stage_relay(chunk):
        if chunk % 2 == 0:
            to_right(chunk).wait_recv()
        else:
            to_left(chunk).wait_recv()
        onward(chunk).start()

    def stage_end(chunk):
        if chunk % 2 == 0:
            to_left(chunk).wait_recv()
        else:
            to_right(chunk).wait_recv()
        onward(chunk).wait_recv()
        start, count = CHUNKS[chunk]
        piece, matrices, lanes = moments.shape[1], theta.shape[1], moments.shape[-1]
        for block in range(REPS):
            lines = pl.ds(block * piece + start, count)
            for tile in range(moments.shape[3]):
                cut = pl.ds(tile * lanes, lanes)
                moment = moments[block, pl.ds(start, count), :, tile].astype(jnp.float32)
                moment = moment.reshape(count, matrices, lanes)
                grad = outer[lines, :, cut]
                renewed = momentum_rate * moment + grad
                update = (outer_rate * (grad + momentum_rate * renewed)).astype(jnp.bfloat16)
                out_ref[lines, :, cut] = (
                    theta[lines, :, cut].astype(jnp.float32) - update.astype(jnp.float32)
                ).astype(jnp.bfloat16)

    half = comp.shape[1]

    def project():
        deltas_copy.wait()
        basis = basis_ref[...]
        nothing = jnp.zeros_like(basis)
        dims = (((1,), (1,)), ((), ()))
        upper = jnp.concatenate([basis, nothing], axis=0)
        lower = jnp.concatenate([nothing, basis], axis=0)
        comp[rep] = (
            lax.dot_general(deltas[:half], upper, dims, preferred_element_type=jnp.float32)
            + lax.dot_general(deltas[half:], lower, dims, preferred_element_type=jnp.float32)
        ).astype(jnp.bfloat16)
        for way in range(3):
            c_copy(way).start()

    def expand():
        for way in range(3):
            c_copy(way).wait()
        theta_copy.wait()
        summed = comp[0].astype(jnp.float32)
        for block in range(1, REPS):
            summed += comp[block].astype(jnp.float32)
        averaged = summed / REPS
        high = averaged.astype(jnp.bfloat16)
        low = (averaged - high.astype(jnp.float32)).astype(jnp.bfloat16)
        both = jnp.concatenate([high, low], axis=1)
        basis = basis_ref[...]
        nothing = jnp.zeros_like(basis)
        rows, matrices, width = theta.shape
        for part in range(2):
            pair = [basis, nothing] if part == 0 else [nothing, basis]
            stacked = jnp.concatenate(pair + pair, axis=0)
            outer[pl.ds(part * rows // 2, rows // 2)] = jnp.dot(
                both, stacked, preferred_element_type=jnp.float32
            ).reshape(rows // 2, matrices, width)

    for chunk in range(total):
        stage_core(chunk)
        if 1 <= chunk <= WINDOW:
            stage_x(chunk - 1)
    if WINDOW == total:
        stage_x(total - 1)
    project()
    for tick in range(total + 3):
        if tick < total:
            stage_z(tick)
            if tick + WINDOW < total:
                stage_x(tick + WINDOW)
        if tick == 1:
            expand()
        if 0 <= tick - 1 < total:
            stage_y(tick - 1)
        if 0 <= tick - 2 < total:
            stage_relay(tick - 2)
        if 0 <= tick - 3 < total:
            stage_end(tick - 3)
    for chunk in range(total):
        core_copy(chunk).wait_send()
        for step in range(1, WIDE):
            x_copy(chunk, step).wait_send()
        for step in range(1, DEPTH):
            z_copy(chunk, step).wait_send()
        to_right(chunk).wait_send()
        to_left(chunk).wait_send()
        onward(chunk).wait_send()


def routed(caps, number, table, moment, deltas, basis_t, theta):
    chip_cap, row_cap = caps
    slots, _, _, _, piece, tiles, lanes = moment.shape
    matrices = theta.shape[1]
    half = deltas.shape[0] // 2
    chunks = len(CHUNKS)
    anywhere = pl.BlockSpec(memory_space=pl.ANY)
    vmem = pl.BlockSpec(memory_space=pltpu.VMEM)

    def buffers(dtype, *lead):
        return [pltpu.VMEM(lead + (n, tiles, lanes), dtype) for _, n in CHUNKS]

    def pair(*shape):
        return [pltpu.SemaphoreType.DMA(shape), pltpu.SemaphoreType.DMA(shape)]

    return pl.pallas_call(
        functools.partial(route, chip_cap, row_cap),
        name="route_%d_%d" % caps,
        out_shape=jax.ShapeDtypeStruct(theta.shape, jnp.bfloat16),
        in_specs=[pl.BlockSpec(memory_space=pltpu.SMEM), anywhere, anywhere, vmem, anywhere],
        out_specs=vmem,
        scratch_shapes=[
            buffers(jnp.float32, slots, DEPTH, WIDE, CORES),
            buffers(jnp.bfloat16, slots, WIDE, DEPTH),
            buffers(jnp.bfloat16, CORES * slots, WIDE, DEPTH),
            buffers(jnp.bfloat16, WIDE, chip_cap, DEPTH),
            buffers(jnp.bfloat16, WIDE * chip_cap, DEPTH),
            buffers(jnp.bfloat16, DEPTH, row_cap),
            buffers(jnp.bfloat16, DEPTH * row_cap),
            pltpu.VMEM((REPS, piece, matrices // 8, tiles, 8, lanes), jnp.bfloat16),
            pltpu.VMEM((REPS, half, 2 * basis_t.shape[0]), jnp.bfloat16),
            pltpu.VMEM(deltas.shape, jnp.bfloat16),
            pltpu.VMEM(theta.shape, jnp.bfloat16),
            pltpu.VMEM(theta.shape, jnp.float32),
            pltpu.SemaphoreType.DMA((chunks + 2,)),
            *pair(chunks),
            *pair(chunks, WIDE - 1),
            *pair(chunks, DEPTH - 1),
            *pair(chunks, 3),
            *pair(3),
        ],
        compiler_params=pltpu.CompilerParams(
            collective_id=number, has_side_effects=True, vmem_limit_bytes=56 << 20
        ),
    )(table, moment, deltas, basis_t, theta)


def arrange(per_chip, per_row, matrices, slot_ref, table_ref, which_ref):
    dev = lax.axis_index("dev")
    entries = slot_ref.shape[1]
    square = (entries, entries)
    across = jnp.broadcast_to(slot_ref[...], square)
    down = across.T
    place = lax.broadcasted_iota(jnp.int32, square, 0)
    line = lax.broadcasted_iota(jnp.int32, square, 1)
    chip, row = place // per_chip, place // per_row
    before = (across >= 0) & (line < place)
    in_chip = jnp.sum(jnp.where(before & (line // per_chip == chip), 1, 0), axis=1, keepdims=True)
    in_row = jnp.sum(jnp.where(before & (line // per_row == row), 1, 0), axis=1, keepdims=True)
    filled = down >= 0
    of_chip, of_row = line < per_chip, line < per_chip + per_row
    in_mine = (chip == dev // CORES) & (in_chip == line)
    in_line = (row == dev // (CORES * WIDE)) & (in_row == line - per_chip)
    held = down == line - per_chip - per_row
    value = jnp.where(
        of_chip,
        jnp.where(filled & in_mine, place % per_chip, 0),
        jnp.where(
            of_row,
            jnp.where(filled & in_line, chip % WIDE * per_chip + in_chip, 0),
            jnp.where(filled & held, row * per_row + in_row, 0),
        ),
    )
    table_ref[...] = jnp.sum(value, axis=0, keepdims=True)
    needed = jnp.zeros(square, jnp.int32)
    for chip_cap, row_cap in CAPS[:-1]:
        needed += jnp.where((in_chip >= chip_cap) | (in_row >= row_cap), 1, 0)
    which_ref[0, 0] = jnp.max(jnp.where(filled, needed, 0))


def planned(slot_row, per_chip, per_row, matrices):
    return pl.pallas_call(
        functools.partial(arrange, per_chip, per_row, matrices),
        name="arrange",
        out_shape=(
            jax.ShapeDtypeStruct(slot_row.shape, jnp.int32),
            jax.ShapeDtypeStruct((1, 1), jnp.int32),
        ),
        in_specs=[pl.BlockSpec(memory_space=pltpu.VMEM)],
        out_specs=(pl.BlockSpec(memory_space=pltpu.VMEM), pl.BlockSpec(memory_space=pltpu.SMEM)),
    )(slot_row)


def per_device(theta, deltas, momentum, basis, slot_matrix):
    matrices, rows, width = theta.shape
    slots, dev_count = momentum.shape[0], momentum.shape[1]
    piece = momentum.shape[3]
    entries = slots * dev_count
    per_chip = slots * CORES
    per_row = per_chip * WIDE

    moment = momentum.reshape(slots, DEPTH, WIDE, CORES, piece, width // 128, 128)
    by_row = deltas[0].transpose(1, 0, 2).reshape(rows * matrices, width)

    table, which = planned(slot_matrix.reshape(1, entries), per_chip, per_row, matrices)

    def branch(number):
        return lambda: routed(
            CAPS[number], number, table, moment, by_row, basis.T, theta.transpose(1, 0, 2)
        )

    return lax.switch(which.reshape(()), [branch(n) for n in range(len(CAPS))]).transpose(1, 0, 2)


def solution(mesh):
    placed = (
        P(None, "dev", None),
        P("rep", None, "dev", None),
        P("dev", None, "rep", None, None),
        P(),
        P(),
    )
    return jax.shard_map(
        per_device, mesh=mesh, in_specs=placed, out_specs=P(None, "dev", None), check_vma=False,
    )
```
